32 devices in a mesh: doc: 8 (over y, x, core), head: 4 (over z).
Axes of the slice: x: 2, y: 2, z: 4, core: 2. Of those that a mesh axis runs over, the one named last changes fastest.
Arguments:
- queries: bfloat16 [2048, 2048], P(('doc', 'head')), may hold values from -6 to 6
- keys: bfloat16 [2048, 2048], P(('doc', 'head')), may hold values from -6 to 6
- values: bfloat16 [2048, 2048], P(('doc', 'head')), may hold values from -6 to 6
- log_decay: bfloat16 [2048, 2048], P(('doc', 'head')), may hold values from -1 to 0
- beta_logit: bfloat16 [2048, 16], P(('doc', 'head')), may hold values from -6 to 6
- block_owner: int32 [8, 16], replicated, may hold values from 0 to 7, as said below
- block_start: int32 [8, 16], replicated, may hold values from 0 to 1, as said below
- gain: float32 [2048], P('head'), may hold values from 0.25 to 1.75
Outputs:
- attended: bfloat16 [4096, 2048], P('doc', 'head')
The draws below stay inside these ranges and needn't reach their ends.
Inputs may be any that keep to these rules, and one draw needn't show every extreme that they name: `block_owner`: every block of index d of doc goes to owner (d + k) mod 8 for some k from 0 to 3; the blocks of one index with one owner form one run; a document lies in one run; at most 8 blocks of one index go to one owner, and exactly 8 to some owner of every index. `block_start`: the first block of every run of block_owner is 1; a document has 1 to 8 blocks.
All inputs are finite; a program needn't handle non-finite values.
Results may differ from the reference program's by a relative error of at most 0.001.
Values may be sent and summed in bfloat16 or wider, within the bound.
A program may use at most 64 MiB of HBM per device.

```python
import math
import jax
import jax.numpy as jnp
from jax import lax

PER_QUERY_WIDTH = 128
OWNED_PARTITION = 16
ALL_WIDTH_SUM = 2048
TOK_DEV = 64
BLOCK = 16
TILE = 128
RUNS = 4
ROWTOK = 256
RB = 16
CAP = 8
OS = 512
SEQUENCE_LENGTH = 2048
N_DOC = 8


def block_lists(floor_value):
    mean = RB // RUNS

    def one_row(row_key, row_index):
        parts_keys = jax.random.split(row_key, 5)
        order = jax.random.permutation(parts_keys[0], RUNS)
        delta = jax.random.randint(parts_keys[1], (RUNS // 2,), -mean, mean + 1)
        forced = jax.random.randint(parts_keys[2], (), 0, RUNS // 2)
        delta = jnp.where(jnp.arange(RUNS // 2) == forced, mean, delta)
        lengths = jnp.stack([mean + delta, mean - delta], axis=1).reshape(RUNS)
        ends = jnp.cumsum(lengths)
        begins = ends - lengths
        blocks = jnp.arange(RB)
        which = jnp.sum((blocks[:, None] >= ends[None, :]).astype(jnp.int32), axis=1)
        owner = jnp.mod(row_index + order[which], N_DOC)
        place = blocks - begins[which]
        cutting = jax.random.randint(parts_keys[3], (RUNS,), 1, max(2 * mean, 2))
        splits = jax.random.randint(parts_keys[4], (RUNS,), 0, 2)
        starts = (place == 0) | (splits[which] == 1) & (place == cutting[which])
        return (owner.astype(jnp.int32), starts.astype(jnp.int32))
    shared = jax.random.fold_in(floor_value, 7)
    row_keys = jax.vmap(lambda index: jax.random.fold_in(shared, index))(jnp.arange(N_DOC))
    return jax.vmap(one_row)(row_keys, jnp.arange(N_DOC, dtype=jnp.int32))


def draw_block_owner(key, part):
    return block_lists(key)[0]


def draw_block_start(key, part):
    return block_lists(key)[1]


def draw_log_decay(key, part):
    complete_probe_vectors = jax.random.split(key, 5)
    floor_value = jnp.exp(jax.random.uniform(complete_probe_vectors[0], (1, ALL_WIDTH_SUM), minval=math.log(0.003), maxval=math.log(0.08)))
    devices = SEQUENCE_LENGTH // TOK_DEV
    multiplier_coefficient = jnp.exp(jax.random.uniform(complete_probe_vectors[1], (devices, 1, 1), minval=math.log(0.6), maxval=math.log(1.6)))
    multiplier_coefficient = jnp.broadcast_to(multiplier_coefficient, (devices, TOK_DEV, 1)).reshape(SEQUENCE_LENGTH, 1)
    noise_perturbation = jnp.exp(jax.random.uniform(complete_probe_vectors[2], (SEQUENCE_LENGTH, ALL_WIDTH_SUM), minval=-0.5, maxval=0.5))
    spike_occurrence = jax.random.uniform(complete_probe_vectors[3], (SEQUENCE_LENGTH, OWNED_PARTITION, 1)) < 0.006
    dispersion_width = jax.random.uniform(complete_probe_vectors[4], (SEQUENCE_LENGTH, OWNED_PARTITION, 1), minval=math.log(0.5), maxval=math.log(0.8))
    spike_occurrences = jnp.broadcast_to(jnp.where(spike_occurrence, dispersion_width, 0.0), (SEQUENCE_LENGTH, OWNED_PARTITION, PER_QUERY_WIDTH)).reshape(SEQUENCE_LENGTH, ALL_WIDTH_SUM)
    return (spike_occurrences - floor_value * multiplier_coefficient * noise_perturbation).astype(jnp.float32).astype(jnp.bfloat16)


def level_of(stream_key, shape, pieces, smallest, high):
    def one(dim, shards_of):
        draws = jax.random.uniform(jax.random.fold_in(jax.random.fold_in(stream_key, 6), dim), (shards_of,), jnp.float32, smallest / len(pieces), high / len(pieces))
        return jnp.repeat(jnp.exp(draws), shape[dim] // shards_of).reshape((-1,) + (1,) * (len(shape) - dim - 1))

    level = one(*pieces[0])
    for cut in pieces[1:]:
        level = level * one(*cut)
    return level


def gaussian(stream_key, dims, scale, most, cuts=(), kind=jnp.bfloat16):
    values = scale * jax.random.normal(stream_key, dims, jnp.float32)
    if cuts:
        values = values * level_of(stream_key, dims, cuts, -0.22, 0.18)
    return jnp.clip(values, -most, most).astype(kind)


def setup_inputs(seed: int = 0) -> dict:
    streams_of = jax.random.split(jax.random.key(seed), 9)
    queries = gaussian(streams_of[0], (SEQUENCE_LENGTH, ALL_WIDTH_SUM), 1.0, 6.0, ((0, 32),))
    keys = gaussian(streams_of[1], (SEQUENCE_LENGTH, ALL_WIDTH_SUM), 1.0, 6.0, ((0, 32),))
    values = gaussian(streams_of[2], (SEQUENCE_LENGTH, ALL_WIDTH_SUM), 1.0, 6.0, ((0, 32),))
    log_decay = draw_log_decay(jax.random.fold_in(streams_of[8], 71), 0)
    beta_logit = gaussian(streams_of[4], (SEQUENCE_LENGTH, OWNED_PARTITION), 1.5, 6.0, ((0, 32),))
    block_owner = draw_block_owner(jax.random.fold_in(streams_of[8], 71), 0)
    block_start = draw_block_start(jax.random.fold_in(streams_of[8], 71), 0)
    gain = jnp.clip(1.0 + 0.15 * jax.random.normal(streams_of[7], (ALL_WIDTH_SUM,), jnp.float32), 0.25, 1.75)
    return {"queries": queries, "keys": keys, "values": values, "log_decay": log_decay, "beta_logit": beta_logit, "block_owner": block_owner, "block_start": block_start, "gain": gain}


HIGH = lax.Precision.HIGHEST

def unit_lower_inverse(amat):
    tile = amat.shape[-1]
    negated = -amat
    inverse = jnp.eye(tile, dtype=jnp.float32)[None] + negated
    power = negated
    for level in range(tile.bit_length() - 2):
        power = jnp.einsum('nts,nsr->ntr', power, power, precision=HIGH)
        inverse = inverse + jnp.einsum('nts,nsr->ntr', inverse, power, precision=HIGH)
    return inverse

def recurrence(query, key_in, value, decay, beta_raw, start):
    length, width = query.shape
    count = length // TILE
    query_f = query.astype(jnp.float32)
    keys_f = key_in.astype(jnp.float32)
    query_f = query_f * lax.rsqrt(lax.optimization_barrier(jnp.sum(query_f * query_f, axis=-1, keepdims=True)) + 1e-06) * width ** (-0.5)
    keys_f = keys_f * lax.rsqrt(lax.optimization_barrier(jnp.sum(keys_f * keys_f, axis=-1, keepdims=True)) + 1e-06)
    query_f = query_f.reshape(count, TILE, width)
    keys_f = keys_f.reshape(count, TILE, width)
    values_f = value.astype(jnp.float32).reshape(count, TILE, width)
    beta = jax.nn.sigmoid(beta_raw.astype(jnp.float32)).reshape(count, TILE, 1)
    decay_f = decay.astype(jnp.float32).reshape(count, TILE, width)
    row_idx = lax.broadcasted_iota(jnp.int32, (TILE, TILE), 0)
    col_idx = lax.broadcasted_iota(jnp.int32, (TILE, TILE), 1)
    lower_incl = row_idx >= col_idx
    lower_strict = row_idx > col_idx
    cumul = jnp.einsum('ts,nsd->ntd', lower_incl.astype(jnp.float32), decay_f, precision=HIGH)
    segment = jnp.cumsum(start.reshape(count, TILE).astype(jnp.int32), axis=1)
    first = (segment == 0).astype(jnp.float32)[:, :, None]
    last_seg = (segment == segment[:, -1:]).astype(jnp.float32)[:, :, None]
    same = segment[:, :, None] == segment[:, None, :]
    growth = jnp.exp(cumul)
    query_g = query_f * growth
    keys_g = keys_f * growth
    keys_inv = keys_f * jnp.exp(-cumul)
    inner = jnp.einsum('ntd,nsd->nts', keys_g, keys_inv, precision=HIGH)
    amat = jnp.where(same & lower_strict, inner, 0.0) * beta
    scores = jnp.where(same & lower_incl, jnp.einsum('ntd,nsd->nts', query_g, keys_inv, precision=HIGH), 0.0)
    right = jnp.concatenate([beta * values_f, beta * first * keys_g], axis=-1)
    solved = jnp.einsum('nts,nse->nte', unit_lower_inverse(amat), right, precision=HIGH)
    update_free = solved[:, :, :width]
    update_state = solved[:, :, width:]
    keys_end = keys_f * jnp.exp(cumul[:, -1:, :] - cumul) * last_seg
    carry_scale = first[:, -1, :] * growth[:, -1, :]
    transfer = jnp.eye(width, dtype=jnp.float32)[None] * carry_scale[:, :, None] - jnp.einsum('nsd,nse->nde', keys_end, update_state, precision=HIGH)
    offset = jnp.einsum('nsd,nse->nde', keys_end, update_free, precision=HIGH)

    def advance(state, pair):
        return (jnp.dot(pair[0], state, precision=HIGH) + pair[1], state)
    unused, states = lax.scan(advance, jnp.zeros((width, width), jnp.float32), (transfer, offset))
    readout = first * query_g - jnp.einsum('nts,nsd->ntd', scores, update_state, precision=HIGH)
    result = jnp.einsum('ntd,nde->nte', readout, states, precision=HIGH) + jnp.einsum('nts,nse->nte', scores, update_free, precision=HIGH)
    return result.reshape(length, width)

def normalize(result, gain):
    heads_here = result.shape[1]
    scale = lax.rsqrt(lax.optimization_barrier(jnp.mean(result * result, axis=-1, keepdims=True)) + 1e-05)
    normed = result * scale * gain.reshape(1, heads_here, PER_QUERY_WIDTH)
    return normed.reshape(result.shape[0], heads_here * PER_QUERY_WIDTH).astype(jnp.bfloat16)

def reference(queries, keys, values, log_decay, beta_logit, block_owner, block_start, gain):
    first_tok = (jnp.arange(BLOCK) == 0).astype(jnp.int32)
    token_start = (block_start[:, :, None] * first_tok[None, None, :]).reshape(N_DOC, ROWTOK)
    run_heads = jax.vmap(recurrence, in_axes=(1, 1, 1, 1, 1, None), out_axes=1)

    def row_out(items):
        query_row, key_row, value_row, decay_row, beta_row, start_row = items
        shaped = [item.reshape(ROWTOK, OWNED_PARTITION, PER_QUERY_WIDTH) for item in (query_row, key_row, value_row, decay_row)]
        result = run_heads(shaped[0], shaped[1], shaped[2], shaped[3], beta_row, start_row)
        return normalize(result, gain)
    rows_out = lax.map(row_out, (queries.reshape(N_DOC, ROWTOK, ALL_WIDTH_SUM), keys.reshape(N_DOC, ROWTOK, ALL_WIDTH_SUM), values.reshape(N_DOC, ROWTOK, ALL_WIDTH_SUM), log_decay.reshape(N_DOC, ROWTOK, ALL_WIDTH_SUM), beta_logit.reshape(N_DOC, ROWTOK, OWNED_PARTITION), token_start))
    earlier = (jnp.arange(RB)[None, :] < jnp.arange(RB)[:, None]).astype(jnp.int32)
    matches = (block_owner[:, :, None] == block_owner[:, None, :]).astype(jnp.int32)
    ranks = lax.optimization_barrier(jnp.sum(matches * earlier[None], axis=2)).astype(jnp.int32)
    rows_index = jnp.arange(N_DOC, dtype=jnp.int32)[:, None]
    offsets = jnp.mod(block_owner - rows_index + N_DOC, N_DOC).astype(jnp.int32)
    target = (block_owner * (RUNS * CAP) + offsets * CAP + ranks).astype(jnp.int32)
    placed = jnp.zeros((N_DOC * RUNS * CAP, BLOCK, ALL_WIDTH_SUM), jnp.bfloat16)
    placed = placed.at[target.reshape(-1)].set(rows_out.reshape(N_DOC * RB, BLOCK, ALL_WIDTH_SUM))
    return placed.reshape(N_DOC * OS, ALL_WIDTH_SUM)
```

```python
import functools

import jax
import jax.numpy as jnp
from jax import lax
from jax.experimental import pallas as pl
from jax.experimental.pallas import tpu as pltpu
from jax.sharding import PartitionSpec as P

WIDTH = 128
BLOCK = 16
TILE = 128
RUNS = 4
BASE = 8

MESH = pl.DeviceIdType.MESH
F32 = jnp.float32
BF16 = jnp.bfloat16
NN = (((1,), (0,)), ((), ()))
NT = (((1,), (1,)), ((), ()))
TN = (((0,), (0,)), ((), ()))


def split(x):
    high = x.astype(BF16)
    return high, (x - high.astype(F32)).astype(BF16)


def bdot(a, b, dims=NN):
    return lax.dot_general(a, b, dims, preferred_element_type=F32)


def dot3(a, b, dims=NN):
    a_high, a_low = split(a) if not isinstance(a, tuple) else a
    b_high, b_low = split(b) if not isinstance(b, tuple) else b
    ca, cb = dims[0][0][0], dims[0][1][0]
    left = jnp.concatenate([a_high, a_low, a_high], axis=ca)
    right = jnp.concatenate([b_high, b_high, b_low], axis=cb)
    return bdot(left, right, dims)


def lane_iota(shape):
    return lax.broadcasted_iota(jnp.int32, shape, 1)


def row_iota(shape):
    return lax.broadcasted_iota(jnp.int32, shape, 0)


def inverses(mats):
    shape = (TILE, TILE)
    row, col = row_iota(shape), lane_iota(shape)
    eye = (row == col).astype(F32)
    diag = row // BASE == col // BASE
    neg = [jnp.where(diag, -a, 0.0) for a in mats]
    power = [dot3(n, n) for n in neg]
    inv = [eye + n for n in neg]
    size = 2
    while size < BASE:
        last = size * 2 >= BASE
        if last:
            inv = [x + dot3(x, p) for x, p in zip(inv, power)]
        else:
            both = [dot3(jnp.concatenate([x, p], axis=0), p) for x, p in zip(inv, power)]
            inv = [x + b[:TILE] for x, b in zip(inv, both)]
            power = [b[TILE:] for b in both]
        size *= 2
    size = BASE
    while size < TILE:
        off = (row // (2 * size) == col // (2 * size)) & (row // size > col // size)
        parts = [split(x) for x in inv]
        mid = [dot3(jnp.where(off, a, 0.0), x) for a, x in zip(mats, parts)]
        inv = [x - dot3(p, m) for x, p, m in zip(inv, parts, mid)]
        size *= 2
    return inv


def kernel(
    nz, nd, q_ref, k_ref, v_ref, g_ref, b_ref, owner_ref, start_ref, gain_ref, out_ref,
    buf, bbuf, place, stage, segcol, masks,
    send_sem, recv_sem, bsend_sem, brecv_sem, osend_sem, orecv_sem,
):
    me = lax.axis_index("head")
    doc = lax.axis_index("doc")
    heads, _, rowtok, _ = buf.shape
    tok = q_ref.shape[0]
    nblk = rowtok // BLOCK
    cap = 2 * nblk // RUNS
    capt = cap * BLOCK
    tiles = rowtok // TILE
    refs = (q_ref, k_ref, v_ref, g_ref)

    barrier = pltpu.get_barrier_semaphore()
    count = 0
    for step in range(1, nz):
        pl.semaphore_signal(
            barrier, inc=1, device_id={"head": lax.rem(me + step, nz)}, device_id_type=MESH
        )
        count += 1
    peers = sorted({s % nd for s in range(1, RUNS)} | {(-s) % nd for s in range(1, RUNS)})
    for step in peers:
        pl.semaphore_signal(
            barrier, inc=1, device_id={"doc": lax.rem(doc + step, nd)}, device_id_type=MESH
        )
        count += 1
    pl.semaphore_wait(barrier, count)

    mine = pl.ds(pl.multiple_of(me * tok, tok), tok)

    def incoming(step, head, which):
        partner = lax.rem(me + step, nz)
        column = pl.ds(pl.multiple_of((partner * heads + head) * WIDTH, WIDTH), WIDTH)
        source = refs[which].at[:, column]
        target = buf.at[head, which, mine, :]
        if step == 0:
            return pltpu.make_async_copy(source, target, recv_sem.at[0, head, which])
        return pltpu.make_async_remote_copy(
            src_ref=source,
            dst_ref=target,
            send_sem=send_sem.at[step, head, which],
            recv_sem=recv_sem.at[step, head, which],
            device_id={"head": partner},
            device_id_type=MESH,
        )

    def incoming_beta(step):
        if step == 0:
            return pltpu.make_async_copy(b_ref, bbuf.at[me], brecv_sem.at[0])
        return pltpu.make_async_remote_copy(
            src_ref=b_ref,
            dst_ref=bbuf.at[me],
            send_sem=bsend_sem.at[step],
            recv_sem=brecv_sem.at[step],
            device_id={"head": lax.rem(me + step, nz)},
            device_id_type=MESH,
        )

    def outgoing(run, head):
        rows = pl.ds(run * capt, capt)
        return pltpu.make_async_remote_copy(
            src_ref=stage.at[head, rows, :],
            dst_ref=out_ref.at[rows, pl.ds(pl.multiple_of(head * WIDTH, WIDTH), WIDTH)],
            send_sem=osend_sem.at[run, head],
            recv_sem=orecv_sem.at[run, head],
            device_id={"doc": lax.rem(doc + run, nd)},
            device_id_type=MESH,
        )

    for step in range(nz):
        incoming_beta(step).start()
    for head in range(heads):
        for step in list(range(1, nz)) + [0]:
            for which in range(4):
                incoming(step, head, which).start()

    here = row_iota((nd, nblk)) == doc
    owner = jnp.sum(jnp.where(here, owner_ref[...], 0), axis=0, keepdims=True)
    start = jnp.sum(jnp.where(here, start_ref[...], 0), axis=0, keepdims=True)
    eye_b = row_iota((nblk, nblk)) == lane_iota((nblk, nblk))
    owner_col = jnp.sum(jnp.where(eye_b, owner, 0), axis=1, keepdims=True)
    earlier = row_iota((nblk, nblk)) < lane_iota((nblk, nblk))
    rank = jnp.sum(jnp.where(earlier & (owner_col == owner), 1, 0), axis=0, keepdims=True)
    ahead = owner - doc
    ahead = jnp.where(ahead < 0, ahead + nd, ahead)
    slot = (ahead * cap + rank).astype(F32).astype(BF16)
    token_block = lane_iota((nblk, rowtok)) // BLOCK
    expand = (row_iota((nblk, rowtok)) == token_block).astype(F32).astype(BF16)
    slot_tok = bdot(slot, expand).astype(jnp.int32) * BLOCK + lane_iota((1, rowtok)) % BLOCK
    place[...] = (row_iota((RUNS * capt, rowtok)) == slot_tok).astype(F32).astype(BF16)
    upto = (row_iota((nblk, rowtok)) <= token_block).astype(F32).astype(BF16)
    seg_row = bdot(start.astype(F32).astype(BF16), upto)
    seg_col = jnp.sum(
        jnp.where(
            lane_iota((rowtok, nblk)) <= row_iota((rowtok, nblk)) // BLOCK, start.astype(F32), 0.0
        ),
        axis=1,
        keepdims=True,
    )
    segcol[...] = jnp.broadcast_to(seg_col, (rowtok, WIDTH))
    shape = (TILE, TILE)
    for tile in range(tiles):
        lo = tile * TILE
        same = seg_col[lo : lo + TILE] == seg_row[:, lo : lo + TILE]
        masks[tile, 0] = (same & (row_iota(shape) > lane_iota(shape))).astype(F32)
        masks[tile, 1] = (same & (row_iota(shape) >= lane_iota(shape))).astype(F32)

    for step in range(nz):
        if step == 0:
            incoming_beta(0).wait()
        else:
            incoming_beta(step).wait_recv()

    def one_head(head, carry):
        for step in range(nz):
            for which in range(4):
                if step == 0:
                    incoming(0, head, which).wait()
                else:
                    incoming(step, head, which).wait_recv()
        braw = bbuf[...].astype(F32).reshape(rowtok, bbuf.shape[2])
        braw = jnp.sum(
            jnp.where(lane_iota(braw.shape) == me * heads + head, braw, 0.0), axis=1, keepdims=True
        )
        beta = jax.nn.sigmoid(braw)
        lower = (row_iota(shape) >= lane_iota(shape)).astype(F32).astype(BF16)
        amats, scores, qgs, kgs, kes, ems, vs = [], [], [], [], [], [], []
        for tile in range(tiles):
            rows = pl.ds(tile * TILE, TILE)
            query = buf[head, 0, rows, :].astype(F32)
            key = buf[head, 1, rows, :].astype(F32)
            vs.append(buf[head, 2, rows, :].astype(F32))
            query = (
                query
                * lax.rsqrt(jnp.sum(query * query, axis=-1, keepdims=True) + 1e-06)
                * WIDTH ** (-0.5)
            )
            key = key * lax.rsqrt(jnp.sum(key * key, axis=-1, keepdims=True) + 1e-06)
            cumul = bdot(lower, buf[head, 3, rows, :])
            half = 0.5 * cumul[TILE - 1 :, :]
            grow = jnp.exp(cumul - half)
            shrink = jnp.exp(half - cumul)
            ems.append(jnp.exp(half))
            qg, kg, ki = query * grow, key * grow, key * shrink
            both = dot3(jnp.concatenate([kg, qg], axis=0), ki, NT)
            b = beta[tile * TILE : (tile + 1) * TILE]
            amats.append(jnp.where(masks[tile, 0] > 0.0, both[:TILE], 0.0) * b)
            scores.append(jnp.where(masks[tile, 1] > 0.0, both[TILE:], 0.0))
            qgs.append(qg)
            kgs.append(kg)
            kes.append(ki)
        invs = inverses(amats)
        state = None
        outs = []
        for tile in range(tiles):
            lo = tile * TILE
            b = beta[lo : lo + TILE]
            seg = segcol[lo : lo + TILE, :]
            right = vs[tile]
            if tile > 0:
                first = (seg == segcol[lo - 1 : lo, :]).astype(F32) * ems[tile]
                both = dot3(
                    jnp.concatenate([kgs[tile] * first, qgs[tile] * first], axis=0), state
                )
                right = right - both[:TILE]
            update = split(dot3(invs[tile], b * right))
            result = dot3(scores[tile], update)
            if tile > 0:
                result = result + both[TILE:]
            if tile < tiles - 1:
                last = (seg == segcol[lo + TILE - 1 : lo + TILE, :]).astype(F32) * ems[tile]
                added = dot3(kes[tile] * last, update, TN)
                if tile > 0:
                    scale = ems[tile] * ems[tile] * (
                        segcol[lo + TILE - 1 : lo + TILE, :] == segcol[lo - 1 : lo, :]
                    ).astype(F32)
                    eye = row_iota(shape) == lane_iota(shape)
                    scale = jnp.sum(jnp.where(eye, scale, 0.0), axis=1, keepdims=True)
                    added = added + scale * state
                state = added
            norm = lax.rsqrt(jnp.mean(result * result, axis=-1, keepdims=True) + 1e-05)
            gain = gain_ref[:, pl.ds(pl.multiple_of(head * WIDTH, WIDTH), WIDTH)]
            outs.append((result * norm * gain).astype(BF16))
        placed = bdot(place[...], jnp.concatenate(outs, axis=0)).astype(BF16)
        stage[head] = placed
        for run in range(1, RUNS):
            outgoing(run, head).start()
        out_ref[0:capt, pl.ds(pl.multiple_of(head * WIDTH, WIDTH), WIDTH)] = placed[:capt]
        return carry

    lax.fori_loop(0, heads, one_head, 0)

    def finish(head, carry):
        for step in range(1, nz):
            for which in range(4):
                incoming(step, head, which).wait_send()
        for run in range(1, RUNS):
            outgoing(run, head).wait()
        return carry

    for step in range(1, nz):
        incoming_beta(step).wait_send()
    lax.fori_loop(0, heads, finish, 0)


def solution(mesh):
    nz, nd = mesh.shape["head"], mesh.shape["doc"]

    def local(queries, keys, values, log_decay, beta_logit, block_owner, block_start, gain):
        tok, channels = queries.shape
        heads = channels // WIDTH // nz
        rowtok = tok * nz
        slots = 2 * rowtok
        vmem = pl.BlockSpec(memory_space=pltpu.VMEM)
        return pl.pallas_call(
            functools.partial(kernel, nz, nd),
            out_shape=jax.ShapeDtypeStruct((slots, heads * WIDTH), BF16),
            in_specs=[vmem] * 8,
            out_specs=vmem,
            scratch_shapes=[
                pltpu.VMEM((heads, 4, rowtok, WIDTH), BF16),
                pltpu.VMEM((nz, tok, beta_logit.shape[1]), BF16),
                pltpu.VMEM((slots, rowtok), BF16),
                pltpu.VMEM((heads, slots, WIDTH), BF16),
                pltpu.VMEM((rowtok, WIDTH), F32),
                pltpu.VMEM((rowtok // TILE, 2, TILE, TILE), F32),
                pltpu.SemaphoreType.DMA((nz, heads, 4)),
                pltpu.SemaphoreType.DMA((nz, heads, 4)),
                pltpu.SemaphoreType.DMA((nz,)),
                pltpu.SemaphoreType.DMA((nz,)),
                pltpu.SemaphoreType.DMA((RUNS, heads)),
                pltpu.SemaphoreType.DMA((RUNS, heads)),
            ],
            compiler_params=pltpu.CompilerParams(
                collective_id=0, has_side_effects=True, vmem_limit_bytes=60 * 1024 * 1024
            ),
            name="delta",
        )(
            queries, keys, values, log_decay, beta_logit, block_owner, block_start,
            gain.reshape(1, -1),
        )

    return jax.shard_map(
        local,
        mesh=mesh,
        in_specs=(P(("doc", "head"), None),) * 5 + (P(), P(), P("head")),
        out_specs=P("doc", "head"),
        check_vma=False,
    )
```

```python
import functools

import jax
import jax.numpy as jnp
from jax import lax
from jax.experimental import pallas as pl
from jax.experimental.pallas import tpu as pltpu
from jax.sharding import PartitionSpec as P

WIDTH = 128
BLOCK = 16
TILE = 128
RUNS = 4
BASE = 16

MESH = pl.DeviceIdType.MESH
F32 = jnp.float32
BF16 = jnp.bfloat16
NN = (((1,), (0,)), ((), ()))
NT = (((1,), (1,)), ((), ()))
TN = (((0,), (0,)), ((), ()))


def split(x):
    high = x.astype(BF16)
    return high, (x - high.astype(F32)).astype(BF16)


def bdot(a, b, dims=NN):
    return lax.dot_general(a, b, dims, preferred_element_type=F32)


def dot3(a, b, dims=NN):
    a_high, a_low = split(a) if not isinstance(a, tuple) else a
    b_high, b_low = split(b) if not isinstance(b, tuple) else b
    ca, cb = dims[0][0][0], dims[0][1][0]
    left = jnp.concatenate([a_high, a_low], axis=ca)
    free = 1 - cb
    top = jnp.concatenate([b_high, b_low], axis=free)
    bottom = jnp.concatenate([b_high, jnp.zeros_like(b_low)], axis=free)
    both = bdot(left, jnp.concatenate([top, bottom], axis=cb), dims)
    width = both.shape[1] // 2
    return both[:, :width] + both[:, width:]


def lane_iota(shape):
    return lax.broadcasted_iota(jnp.int32, shape, 1)


def row_iota(shape):
    return lax.broadcasted_iota(jnp.int32, shape, 0)


def neumann(neg, order, eye):
    power = [dot3(n, n) for n in neg]
    total = [eye + n for n in neg]
    size = 2
    while size < order:
        if size * 2 >= order:
            total = [x + dot3(x, p) for x, p in zip(total, power)]
        else:
            both = [dot3(jnp.concatenate([x, p], axis=0), p) for x, p in zip(total, power)]
            total = [x + b[:TILE] for x, b in zip(total, both)]
            power = [b[TILE:] for b in both]
        size *= 2
    return total


def inverses(mats):
    shape = (TILE, TILE)
    row, col = row_iota(shape), lane_iota(shape)
    eye = (row == col).astype(F32)
    diag = row // BASE == col // BASE
    inner = neumann([jnp.where(diag, -a, 0.0) for a in mats], BASE, eye)
    parts = [split(x) for x in inner]
    outer = [-dot3(p, jnp.where(diag, 0.0, a)) for p, a in zip(parts, mats)]
    return [dot3(y, p) for y, p in zip(neumann(outer, TILE // BASE, eye), parts)]


def kernel(
    nz, nd, q_ref, k_ref, v_ref, g_ref, b_ref, owner_ref, start_ref, gain_ref, out_ref,
    buf, bbuf, betas, place, stage, segcol, masks, growth, keyinv, keystate, keyend, halves,
    inverse, update, states,
    send_sem, recv_sem, bsend_sem, brecv_sem, osend_sem, orecv_sem,
):
    me = lax.axis_index("head")
    doc = lax.axis_index("doc")
    heads, _, rowtok, _ = buf.shape
    tok = q_ref.shape[0]
    nblk = rowtok // BLOCK
    cap = 2 * nblk // RUNS
    capt = cap * BLOCK
    tiles = rowtok // TILE
    refs = (q_ref, k_ref, v_ref, g_ref)

    barrier = pltpu.get_barrier_semaphore()
    count = 0
    for step in range(1, nz):
        pl.semaphore_signal(
            barrier, inc=1, device_id={"head": lax.rem(me + step, nz)}, device_id_type=MESH
        )
        count += 1
    peers = sorted({s % nd for s in range(1, RUNS)} | {(-s) % nd for s in range(1, RUNS)})
    for step in peers:
        pl.semaphore_signal(
            barrier, inc=1, device_id={"doc": lax.rem(doc + step, nd)}, device_id_type=MESH
        )
        count += 1
    pl.semaphore_wait(barrier, count)

    mine = pl.ds(pl.multiple_of(me * tok, tok), tok)

    def incoming(step, head, which):
        partner = lax.rem(me + step, nz)
        column = pl.ds(pl.multiple_of((partner * heads + head) * WIDTH, WIDTH), WIDTH)
        source = refs[which].at[:, column]
        target = buf.at[head, which, mine, :]
        if step == 0:
            return pltpu.make_async_copy(source, target, recv_sem.at[0, head, which])
        return pltpu.make_async_remote_copy(
            src_ref=source,
            dst_ref=target,
            send_sem=send_sem.at[step, head, which],
            recv_sem=recv_sem.at[step, head, which],
            device_id={"head": partner},
            device_id_type=MESH,
        )

    def incoming_beta(step):
        if step == 0:
            return pltpu.make_async_copy(b_ref, bbuf.at[me], brecv_sem.at[0])
        return pltpu.make_async_remote_copy(
            src_ref=b_ref,
            dst_ref=bbuf.at[me],
            send_sem=bsend_sem.at[step],
            recv_sem=brecv_sem.at[step],
            device_id={"head": lax.rem(me + step, nz)},
            device_id_type=MESH,
        )

    def outgoing(run, head):
        rows = pl.ds(run * capt, capt)
        return pltpu.make_async_remote_copy(
            src_ref=stage.at[head, rows, :],
            dst_ref=out_ref.at[rows, pl.ds(pl.multiple_of(head * WIDTH, WIDTH), WIDTH)],
            send_sem=osend_sem.at[run, head],
            recv_sem=orecv_sem.at[run, head],
            device_id={"doc": lax.rem(doc + run, nd)},
            device_id_type=MESH,
        )

    for step in range(nz):
        incoming_beta(step).start()
    for group in ((1, 3), (2,), (0,)):
        for head in range(heads):
            for step in list(range(1, nz)) + [0]:
                for which in group:
                    incoming(step, head, which).start()

    here = row_iota((nd, nblk)) == doc
    owner = jnp.sum(jnp.where(here, owner_ref[...], 0), axis=0, keepdims=True)
    start = jnp.sum(jnp.where(here, start_ref[...], 0), axis=0, keepdims=True)
    eye_b = row_iota((nblk, nblk)) == lane_iota((nblk, nblk))
    owner_col = jnp.sum(jnp.where(eye_b, owner, 0), axis=1, keepdims=True)
    earlier = row_iota((nblk, nblk)) < lane_iota((nblk, nblk))
    rank = jnp.sum(jnp.where(earlier & (owner_col == owner), 1, 0), axis=0, keepdims=True)
    ahead = owner - doc
    ahead = jnp.where(ahead < 0, ahead + nd, ahead)
    slot = (ahead * cap + rank).astype(F32).astype(BF16)
    token_block = lane_iota((nblk, rowtok)) // BLOCK
    expand = (row_iota((nblk, rowtok)) == token_block).astype(F32).astype(BF16)
    slot_tok = bdot(slot, expand).astype(jnp.int32) * BLOCK + lane_iota((1, rowtok)) % BLOCK
    place[...] = (row_iota((RUNS * capt, rowtok)) == slot_tok).astype(F32).astype(BF16)
    upto = (row_iota((nblk, rowtok)) <= token_block).astype(F32).astype(BF16)
    seg_row = bdot(start.astype(F32).astype(BF16), upto)
    seg_col = jnp.sum(
        jnp.where(
            lane_iota((rowtok, nblk)) <= row_iota((rowtok, nblk)) // BLOCK, start.astype(F32), 0.0
        ),
        axis=1,
        keepdims=True,
    )
    segcol[...] = jnp.broadcast_to(seg_col, (rowtok, WIDTH))
    shape = (TILE, TILE)
    for tile in range(tiles):
        lo = tile * TILE
        same = seg_col[lo : lo + TILE] == seg_row[:, lo : lo + TILE]
        masks[tile, 0] = (same & (row_iota(shape) > lane_iota(shape))).astype(F32)
        masks[tile, 1] = (same & (row_iota(shape) >= lane_iota(shape))).astype(F32)

    for step in range(nz):
        if step == 0:
            incoming_beta(0).wait()
        else:
            incoming_beta(step).wait_recv()

    eye_tok = (row_iota((tok, tok)) == lane_iota((tok, tok))).astype(F32).astype(BF16)
    for step in range(nz):
        turned = bdot(eye_tok, bbuf[step], NT)
        betas[step * tok : (step + 1) * tok, :] = jax.nn.sigmoid(turned)

    def arrive(head, which):
        incoming(0, head, which).wait()
        for step in range(1, nz):
            incoming(step, head, which).wait_recv()

    def beta_of(head):
        values = betas[...]
        mine_here = lane_iota(values.shape) == me * heads + head
        return jnp.sum(jnp.where(mine_here, values, 0.0), axis=1, keepdims=True)

    def before(tile):
        return segcol[tile * TILE - 1 : tile * TILE, :]

    def final(tile):
        return segcol[(tile + 1) * TILE - 1 : (tile + 1) * TILE, :]

    group = 2 if heads % 2 == 0 else 1

    def keys_part(index, carry):
        lower = (row_iota(shape) >= lane_iota(shape)).astype(F32).astype(BF16)
        where, amats = [], []
        for member in range(group):
            head = index * group + member
            arrive(head, 1)
            arrive(head, 3)
            beta = beta_of(head)
            for tile in range(tiles):
                rows = pl.ds(tile * TILE, TILE)
                seg = segcol[rows, :]
                key = buf[head, 1, rows, :].astype(F32)
                key = key * lax.rsqrt(jnp.sum(key * key, axis=-1, keepdims=True) + 1e-06)
                cumul = bdot(lower, buf[head, 3, rows, :])
                half = 0.5 * cumul[TILE - 1 :, :]
                grow = jnp.exp(cumul - half)
                middle = jnp.exp(half)
                kg, ki = key * grow, key * jnp.exp(half - cumul)
                amat = dot3(kg, ki, NT)
                amat = jnp.where(masks[tile, 0] > 0.0, amat, 0.0)
                amats.append(amat * beta[tile * TILE : (tile + 1) * TILE])
                where.append((head, rows))
                growth[head, rows, :] = grow
                keyinv[head, rows, :] = ki
                halves[head, tile] = jnp.broadcast_to(middle, (8, WIDTH))
                if tile > 0:
                    keystate[head, rows, :] = kg * ((seg == before(tile)).astype(F32) * middle)
                if tile < tiles - 1:
                    keyend[head, rows, :] = ki * ((seg == final(tile)).astype(F32) * middle)
        for (head, rows), inv in zip(where, inverses(amats)):
            inverse[head, rows, :] = inv
        return carry

    lax.fori_loop(0, heads // group, keys_part, 0)

    def values_part(index, carry):
        members = [index * group + member for member in range(group)]
        state = [None] * group
        for head in members:
            arrive(head, 2)
        beta = [beta_of(head) for head in members]
        for tile in range(tiles):
            lo = tile * TILE
            rows = pl.ds(lo, TILE)
            right = [buf[head, 2, rows, :].astype(F32) for head in members]
            if tile > 0:
                right = [
                    r - dot3(keystate[head, rows, :], s)
                    for r, head, s in zip(right, members, state)
                ]
            new = [
                dot3(inverse[head, rows, :], b[lo : lo + TILE] * r)
                for head, b, r in zip(members, beta, right)
            ]
            for head, n in zip(members, new):
                update[head, rows, :] = n
            if tile < tiles - 1:
                added = [dot3(keyend[head, rows, :], n, TN) for head, n in zip(members, new)]
                if tile > 0:
                    eye = row_iota(shape) == lane_iota(shape)
                    unbroken = (final(tile) == before(tile)).astype(F32)
                    for place_in, head in enumerate(members):
                        middle = halves[head, tile, 0:1, :]
                        scale = middle * middle * unbroken
                        scale = jnp.sum(jnp.where(eye, scale, 0.0), axis=1, keepdims=True)
                        added[place_in] = added[place_in] + scale * state[place_in]
                state = added
                for head, s in zip(members, state):
                    states[head, tile] = s
        return carry

    lax.fori_loop(0, heads // group, values_part, 0)

    def queries_part(head, carry):
        arrive(head, 0)
        gain = gain_ref[:, pl.ds(pl.multiple_of(head * WIDTH, WIDTH), WIDTH)]
        outs = []
        for tile in range(tiles):
            rows = pl.ds(tile * TILE, TILE)
            query = buf[head, 0, rows, :].astype(F32)
            query = (
                query
                * lax.rsqrt(jnp.sum(query * query, axis=-1, keepdims=True) + 1e-06)
                * WIDTH ** (-0.5)
            )
            qg = query * growth[head, rows, :]
            scores = dot3(qg, keyinv[head, rows, :], NT)
            scores = jnp.where(masks[tile, 1] > 0.0, scores, 0.0)
            result = dot3(scores, update[head, rows, :])
            if tile > 0:
                first = (segcol[rows, :] == before(tile)).astype(F32) * halves[head, tile, 0:1, :]
                result = result + dot3(qg * first, states[head, tile - 1])
            norm = lax.rsqrt(jnp.mean(result * result, axis=-1, keepdims=True) + 1e-05)
            outs.append((result * norm * gain).astype(BF16))
        placed = bdot(place[...], jnp.concatenate(outs, axis=0)).astype(BF16)
        stage[head] = placed
        for run in range(1, RUNS):
            outgoing(run, head).start()
        out_ref[0:capt, pl.ds(pl.multiple_of(head * WIDTH, WIDTH), WIDTH)] = placed[:capt]
        return carry

    lax.fori_loop(0, heads, queries_part, 0)

    def finish(head, carry):
        for step in range(1, nz):
            for which in range(4):
                incoming(step, head, which).wait_send()
        for run in range(1, RUNS):
            outgoing(run, head).wait()
        return carry

    for step in range(1, nz):
        incoming_beta(step).wait_send()
    lax.fori_loop(0, heads, finish, 0)


def solution(mesh):
    nz, nd = mesh.shape["head"], mesh.shape["doc"]

    def local(queries, keys, values, log_decay, beta_logit, block_owner, block_start, gain):
        tok, channels = queries.shape
        heads = channels // WIDTH // nz
        rowtok = tok * nz
        slots = 2 * rowtok
        vmem = pl.BlockSpec(memory_space=pltpu.VMEM)
        return pl.pallas_call(
            functools.partial(kernel, nz, nd),
            out_shape=pltpu.VMEM((slots, heads * WIDTH), BF16),
            in_specs=[pl.BlockSpec(memory_space=pl.ANY)] * 4 + [vmem] * 4,
            out_specs=vmem,
            scratch_shapes=[
                pltpu.VMEM((heads, 4, rowtok, WIDTH), BF16),
                pltpu.VMEM((nz, beta_logit.shape[1], tok), BF16),
                pltpu.VMEM((rowtok, beta_logit.shape[1]), F32),
                pltpu.VMEM((slots, rowtok), BF16),
                pltpu.VMEM((heads, slots, WIDTH), BF16),
                pltpu.VMEM((rowtok, WIDTH), F32),
                pltpu.VMEM((rowtok // TILE, 2, TILE, TILE), F32),
                pltpu.VMEM((heads, rowtok, WIDTH), F32),
                pltpu.VMEM((heads, rowtok, WIDTH), F32),
                pltpu.VMEM((heads, rowtok, WIDTH), F32),
                pltpu.VMEM((heads, rowtok, WIDTH), F32),
                pltpu.VMEM((heads, rowtok // TILE, 8, WIDTH), F32),
                pltpu.VMEM((heads, rowtok, WIDTH), F32),
                pltpu.VMEM((heads, rowtok, WIDTH), F32),
                pltpu.VMEM((heads, rowtok // TILE, WIDTH, WIDTH), F32),
                pltpu.SemaphoreType.DMA((nz, heads, 4)),
                pltpu.SemaphoreType.DMA((nz, heads, 4)),
                pltpu.SemaphoreType.DMA((nz,)),
                pltpu.SemaphoreType.DMA((nz,)),
                pltpu.SemaphoreType.DMA((RUNS, heads)),
                pltpu.SemaphoreType.DMA((RUNS, heads)),
            ],
            compiler_params=pltpu.CompilerParams(
                collective_id=0, has_side_effects=True, vmem_limit_bytes=60 * 1024 * 1024
            ),
            name="delta",
        )(
            queries, keys, values, log_decay, beta_logit.T, block_owner, block_start,
            gain.reshape(1, -1),
        )

    return jax.shard_map(
        local,
        mesh=mesh,
        in_specs=(P(("doc", "head"), None),) * 5 + (P(), P(), P("head")),
        out_specs=P("doc", "head"),
        check_vma=False,
    )
```

```python
import functools

import jax
import jax.numpy as jnp
from jax import lax
from jax.experimental import pallas as pl
from jax.experimental.pallas import tpu as pltpu
from jax.sharding import PartitionSpec as P

WIDTH = 128
BLOCK = 16
TILE = 128
RUNS = 4
BASE = 16

MESH = pl.DeviceIdType.MESH
F32 = jnp.float32
BF16 = jnp.bfloat16
NN = (((1,), (0,)), ((), ()))
NT = (((1,), (1,)), ((), ()))
TN = (((0,), (0,)), ((), ()))


def split(x):
    high = x.astype(BF16)
    return high, (x - high.astype(F32)).astype(BF16)


def bdot(a, b, dims=NN):
    return lax.dot_general(a, b, dims, preferred_element_type=F32)


def dot3(a, b, dims=NN):
    a_high, a_low = split(a) if not isinstance(a, tuple) else a
    b_high, b_low = split(b) if not isinstance(b, tuple) else b
    ca, cb = dims[0][0][0], dims[0][1][0]
    left = jnp.concatenate([a_high, a_low], axis=ca)
    free = 1 - cb
    top = jnp.concatenate([b_high, b_low], axis=free)
    bottom = jnp.concatenate([b_high, jnp.zeros_like(b_low)], axis=free)
    both = bdot(left, jnp.concatenate([top, bottom], axis=cb), dims)
    width = both.shape[1] // 2
    return both[:, :width] + both[:, width:]


def lane_iota(shape):
    return lax.broadcasted_iota(jnp.int32, shape, 1)


def row_iota(shape):
    return lax.broadcasted_iota(jnp.int32, shape, 0)


def neumann(neg, order, eye):
    power = [dot3(n, n) for n in neg]
    total = [eye + n for n in neg]
    size = 2
    while size < order:
        if size * 2 >= order:
            total = [x + dot3(x, p) for x, p in zip(total, power)]
        else:
            both = [dot3(jnp.concatenate([x, p], axis=0), p) for x, p in zip(total, power)]
            total = [x + b[:TILE] for x, b in zip(total, both)]
            power = [b[TILE:] for b in both]
        size *= 2
    return total


def inverses(mats):
    shape = (TILE, TILE)
    row, col = row_iota(shape), lane_iota(shape)
    eye = (row == col).astype(F32)
    diag = row // BASE == col // BASE
    inner = neumann([jnp.where(diag, -a, 0.0) for a in mats], BASE, eye)
    parts = [split(x) for x in inner]
    outer = [-dot3(p, jnp.where(diag, 0.0, a)) for p, a in zip(parts, mats)]
    return [dot3(y, p) for y, p in zip(neumann(outer, TILE // BASE, eye), parts)]


def kernel(
    nz, nd, q_ref, k_ref, v_ref, g_ref, b_ref, owner_ref, start_ref, gain_ref, out_ref,
    buf, bbuf, betas, place, stage, segcol, masks, growth, keyinv, keystate, keyend, halves,
    inverse, update, states,
    send_sem, recv_sem, bsend_sem, brecv_sem, osend_sem, orecv_sem,
):
    me = lax.axis_index("head")
    doc = lax.axis_index("doc")
    heads, _, rowtok, _ = buf.shape
    tok = q_ref.shape[0]
    nblk = rowtok // BLOCK
    cap = 2 * nblk // RUNS
    capt = cap * BLOCK
    tiles = rowtok // TILE
    refs = (q_ref, k_ref, v_ref, g_ref)

    barrier = pltpu.get_barrier_semaphore()
    count = 0
    for step in range(1, nz):
        pl.semaphore_signal(
            barrier, inc=1, device_id={"head": lax.rem(me + step, nz)}, device_id_type=MESH
        )
        count += 1
    peers = sorted({s % nd for s in range(1, RUNS)} | {(-s) % nd for s in range(1, RUNS)})
    for step in peers:
        pl.semaphore_signal(
            barrier, inc=1, device_id={"doc": lax.rem(doc + step, nd)}, device_id_type=MESH
        )
        count += 1
    pl.semaphore_wait(barrier, count)

    mine = pl.ds(pl.multiple_of(me * tok, tok), tok)

    def incoming(step, head, which):
        partner = lax.rem(me + step, nz)
        column = pl.ds(pl.multiple_of((partner * heads + head) * WIDTH, WIDTH), WIDTH)
        source = refs[which].at[:, column]
        target = buf.at[head, which, mine, :]
        if step == 0:
            return pltpu.make_async_copy(source, target, recv_sem.at[0, head, which])
        return pltpu.make_async_remote_copy(
            src_ref=source,
            dst_ref=target,
            send_sem=send_sem.at[step, head, which],
            recv_sem=recv_sem.at[step, head, which],
            device_id={"head": partner},
            device_id_type=MESH,
        )

    def incoming_beta(step):
        if step == 0:
            return pltpu.make_async_copy(b_ref, bbuf.at[me], brecv_sem.at[0])
        return pltpu.make_async_remote_copy(
            src_ref=b_ref,
            dst_ref=bbuf.at[me],
            send_sem=bsend_sem.at[step],
            recv_sem=brecv_sem.at[step],
            device_id={"head": lax.rem(me + step, nz)},
            device_id_type=MESH,
        )

    def outgoing(run, head):
        rows = pl.ds(run * capt, capt)
        return pltpu.make_async_remote_copy(
            src_ref=stage.at[head, rows, :],
            dst_ref=out_ref.at[rows, pl.ds(pl.multiple_of(head * WIDTH, WIDTH), WIDTH)],
            send_sem=osend_sem.at[run, head],
            recv_sem=orecv_sem.at[run, head],
            device_id={"doc": lax.rem(doc + run, nd)},
            device_id_type=MESH,
        )

    for step in range(nz):
        incoming_beta(step).start()
    early = max(heads - 2, 0)
    order = [(head, which) for head in range(heads) for which in (1, 3)]
    order += [(head, which) for head in range(early) for which in (2, 0)]
    order += [(head, which) for which in (2, 0) for head in range(early, heads)]
    for head, which in order:
        for step in list(range(1, nz)) + [0]:
            incoming(step, head, which).start()

    here = row_iota((nd, nblk)) == doc
    owner = jnp.sum(jnp.where(here, owner_ref[...], 0), axis=0, keepdims=True)
    start = jnp.sum(jnp.where(here, start_ref[...], 0), axis=0, keepdims=True)
    eye_b = row_iota((nblk, nblk)) == lane_iota((nblk, nblk))
    owner_col = jnp.sum(jnp.where(eye_b, owner, 0), axis=1, keepdims=True)
    earlier = row_iota((nblk, nblk)) < lane_iota((nblk, nblk))
    rank = jnp.sum(jnp.where(earlier & (owner_col == owner), 1, 0), axis=0, keepdims=True)
    ahead = owner - doc
    ahead = jnp.where(ahead < 0, ahead + nd, ahead)
    slot = (ahead * cap + rank).astype(F32).astype(BF16)
    token_block = lane_iota((nblk, rowtok)) // BLOCK
    expand = (row_iota((nblk, rowtok)) == token_block).astype(F32).astype(BF16)
    slot_tok = bdot(slot, expand).astype(jnp.int32) * BLOCK + lane_iota((1, rowtok)) % BLOCK
    place[...] = (row_iota((RUNS * capt, rowtok)) == slot_tok).astype(F32).astype(BF16)
    upto = (row_iota((nblk, rowtok)) <= token_block).astype(F32).astype(BF16)
    seg_row = bdot(start.astype(F32).astype(BF16), upto)
    seg_col = jnp.sum(
        jnp.where(
            lane_iota((rowtok, nblk)) <= row_iota((rowtok, nblk)) // BLOCK, start.astype(F32), 0.0
        ),
        axis=1,
        keepdims=True,
    )
    segcol[...] = jnp.broadcast_to(seg_col, (rowtok, WIDTH))
    shape = (TILE, TILE)
    for tile in range(tiles):
        lo = tile * TILE
        same = seg_col[lo : lo + TILE] == seg_row[:, lo : lo + TILE]
        masks[tile, 0] = (same & (row_iota(shape) > lane_iota(shape))).astype(F32)
        masks[tile, 1] = (same & (row_iota(shape) >= lane_iota(shape))).astype(F32)

    for step in range(nz):
        if step == 0:
            incoming_beta(0).wait()
        else:
            incoming_beta(step).wait_recv()

    eye_tok = (row_iota((tok, tok)) == lane_iota((tok, tok))).astype(F32).astype(BF16)
    for step in range(nz):
        turned = bdot(eye_tok, bbuf[step], NT)
        betas[step * tok : (step + 1) * tok, :] = jax.nn.sigmoid(turned)

    def arrive(head, which):
        incoming(0, head, which).wait()
        for step in range(1, nz):
            incoming(step, head, which).wait_recv()

    def beta_of(head):
        values = betas[...]
        mine_here = lane_iota(values.shape) == me * heads + head
        return jnp.sum(jnp.where(mine_here, values, 0.0), axis=1, keepdims=True)

    def before(tile):
        return segcol[tile * TILE - 1 : tile * TILE, :]

    def final(tile):
        return segcol[(tile + 1) * TILE - 1 : (tile + 1) * TILE, :]

    group = 2 if heads % 2 == 0 else 1

    def keys_part(index, carry):
        lower = (row_iota(shape) >= lane_iota(shape)).astype(F32).astype(BF16)
        where, amats = [], []
        for member in range(group):
            head = index * group + member
            arrive(head, 1)
            arrive(head, 3)
            beta = beta_of(head)
            for tile in range(tiles):
                rows = pl.ds(tile * TILE, TILE)
                seg = segcol[rows, :]
                key = buf[head, 1, rows, :].astype(F32)
                key = key * lax.rsqrt(jnp.sum(key * key, axis=-1, keepdims=True) + 1e-06)
                cumul = bdot(lower, buf[head, 3, rows, :])
                half = 0.5 * cumul[TILE - 1 :, :]
                grow = jnp.exp(cumul - half)
                middle = jnp.exp(half)
                kg, ki = key * grow, key * jnp.exp(half - cumul)
                amat = dot3(kg, ki, NT)
                amat = jnp.where(masks[tile, 0] > 0.0, amat, 0.0)
                amats.append(amat * beta[tile * TILE : (tile + 1) * TILE])
                where.append((head, rows))
                growth[head, rows, :] = grow
                keyinv[head, rows, :] = ki
                halves[head, tile] = jnp.broadcast_to(middle, (8, WIDTH))
                if tile > 0:
                    keystate[head, rows, :] = kg * ((seg == before(tile)).astype(F32) * middle)
                if tile < tiles - 1:
                    keyend[head, rows, :] = ki * ((seg == final(tile)).astype(F32) * middle)
        for (head, rows), inv in zip(where, inverses(amats)):
            inverse[head, rows, :] = inv
        return carry

    lax.fori_loop(0, heads // group, keys_part, 0)

    def values_part(index, carry):
        members = [index]
        state = [None]
        for head in members:
            arrive(head, 2)
        beta = [beta_of(head) for head in members]
        for tile in range(tiles):
            lo = tile * TILE
            rows = pl.ds(lo, TILE)
            right = [buf[head, 2, rows, :].astype(F32) for head in members]
            if tile > 0:
                right = [
                    r - dot3(keystate[head, rows, :], s)
                    for r, head, s in zip(right, members, state)
                ]
            new = [
                dot3(inverse[head, rows, :], b[lo : lo + TILE] * r)
                for head, b, r in zip(members, beta, right)
            ]
            for head, n in zip(members, new):
                update[head, rows, :] = n
            if tile < tiles - 1:
                added = [dot3(keyend[head, rows, :], n, TN) for head, n in zip(members, new)]
                if tile > 0:
                    eye = row_iota(shape) == lane_iota(shape)
                    unbroken = (final(tile) == before(tile)).astype(F32)
                    for place_in, head in enumerate(members):
                        middle = halves[head, tile, 0:1, :]
                        scale = middle * middle * unbroken
                        scale = jnp.sum(jnp.where(eye, scale, 0.0), axis=1, keepdims=True)
                        added[place_in] = added[place_in] + scale * state[place_in]
                state = added
                for head, s in zip(members, state):
                    states[head, tile] = s
        return carry


    def queries_part(head, carry):
        arrive(head, 0)
        gain = gain_ref[:, pl.ds(pl.multiple_of(head * WIDTH, WIDTH), WIDTH)]
        outs = []
        for tile in range(tiles):
            rows = pl.ds(tile * TILE, TILE)
            query = buf[head, 0, rows, :].astype(F32)
            query = (
                query
                * lax.rsqrt(jnp.sum(query * query, axis=-1, keepdims=True) + 1e-06)
                * WIDTH ** (-0.5)
            )
            qg = query * growth[head, rows, :]
            scores = dot3(qg, keyinv[head, rows, :], NT)
            scores = jnp.where(masks[tile, 1] > 0.0, scores, 0.0)
            result = dot3(scores, update[head, rows, :])
            if tile > 0:
                first = (segcol[rows, :] == before(tile)).astype(F32) * halves[head, tile, 0:1, :]
                result = result + dot3(qg * first, states[head, tile - 1])
            norm = lax.rsqrt(jnp.mean(result * result, axis=-1, keepdims=True) + 1e-05)
            outs.append((result * norm * gain).astype(BF16))
        placed = bdot(place[...], jnp.concatenate(outs, axis=0)).astype(BF16)
        stage[head] = placed
        for run in range(1, RUNS):
            outgoing(run, head).start()
        out_ref[0:capt, pl.ds(pl.multiple_of(head * WIDTH, WIDTH), WIDTH)] = placed[:capt]
        return carry

    def both_parts(head, carry):
        return queries_part(head, values_part(head, carry))

    lax.fori_loop(0, early, both_parts, 0)
    lax.fori_loop(early, heads, values_part, 0)
    lax.fori_loop(early, heads, queries_part, 0)

    def finish(head, carry):
        for step in range(1, nz):
            for which in range(4):
                incoming(step, head, which).wait_send()
        for run in range(1, RUNS):
            outgoing(run, head).wait()
        return carry

    for step in range(1, nz):
        incoming_beta(step).wait_send()
    lax.fori_loop(0, heads, finish, 0)


def solution(mesh):
    nz, nd = mesh.shape["head"], mesh.shape["doc"]

    def local(queries, keys, values, log_decay, beta_logit, block_owner, block_start, gain):
        tok, channels = queries.shape
        heads = channels // WIDTH // nz
        rowtok = tok * nz
        slots = 2 * rowtok
        vmem = pl.BlockSpec(memory_space=pltpu.VMEM)
        return pl.pallas_call(
            functools.partial(kernel, nz, nd),
            out_shape=pltpu.VMEM((slots, heads * WIDTH), BF16),
            in_specs=[pl.BlockSpec(memory_space=pl.ANY)] * 4 + [vmem] * 4,
            out_specs=vmem,
            scratch_shapes=[
                pltpu.VMEM((heads, 4, rowtok, WIDTH), BF16),
                pltpu.VMEM((nz, beta_logit.shape[1], tok), BF16),
                pltpu.VMEM((rowtok, beta_logit.shape[1]), F32),
                pltpu.VMEM((slots, rowtok), BF16),
                pltpu.VMEM((heads, slots, WIDTH), BF16),
                pltpu.VMEM((rowtok, WIDTH), F32),
                pltpu.VMEM((rowtok // TILE, 2, TILE, TILE), F32),
                pltpu.VMEM((heads, rowtok, WIDTH), F32),
                pltpu.VMEM((heads, rowtok, WIDTH), F32),
                pltpu.VMEM((heads, rowtok, WIDTH), F32),
                pltpu.VMEM((heads, rowtok, WIDTH), F32),
                pltpu.VMEM((heads, rowtok // TILE, 8, WIDTH), F32),
                pltpu.VMEM((heads, rowtok, WIDTH), F32),
                pltpu.VMEM((heads, rowtok, WIDTH), F32),
                pltpu.VMEM((heads, rowtok // TILE, WIDTH, WIDTH), F32),
                pltpu.SemaphoreType.DMA((nz, heads, 4)),
                pltpu.SemaphoreType.DMA((nz, heads, 4)),
                pltpu.SemaphoreType.DMA((nz,)),
                pltpu.SemaphoreType.DMA((nz,)),
                pltpu.SemaphoreType.DMA((RUNS, heads)),
                pltpu.SemaphoreType.DMA((RUNS, heads)),
            ],
            compiler_params=pltpu.CompilerParams(
                collective_id=0, has_side_effects=True, vmem_limit_bytes=60 * 1024 * 1024
            ),
            name="delta",
        )(
            queries, keys, values, log_decay, beta_logit.T, block_owner, block_start,
            gain.reshape(1, -1),
        )

    return jax.shard_map(
        local,
        mesh=mesh,
        in_specs=(P(("doc", "head"), None),) * 5 + (P(), P(), P("head")),
        out_specs=P("doc", "head"),
        check_vma=False,
    )
```

```python
import functools

import jax
import jax.numpy as jnp
from jax import lax
from jax.experimental import pallas as pl
from jax.experimental.pallas import tpu as pltpu
from jax.sharding import PartitionSpec as P

WIDTH = 128
BLOCK = 16
TILE = 128
RUNS = 4
BASE = 16

MESH = pl.DeviceIdType.MESH
F32 = jnp.float32
BF16 = jnp.bfloat16
NN = (((1,), (0,)), ((), ()))
NT = (((1,), (1,)), ((), ()))
TN = (((0,), (0,)), ((), ()))


def split(x):
    high = x.astype(BF16)
    return high, (x - high.astype(F32)).astype(BF16)


def bdot(a, b, dims=NN):
    return lax.dot_general(a, b, dims, preferred_element_type=F32)


def dot3(a, b, dims=NN):
    a_high, a_low = split(a) if not isinstance(a, tuple) else a
    b_high, b_low = split(b) if not isinstance(b, tuple) else b
    ca, cb = dims[0][0][0], dims[0][1][0]
    left = jnp.concatenate([a_high, a_low], axis=ca)
    free = 1 - cb
    top = jnp.concatenate([b_high, b_low], axis=free)
    bottom = jnp.concatenate([b_high, jnp.zeros_like(b_low)], axis=free)
    both = bdot(left, jnp.concatenate([top, bottom], axis=cb), dims)
    width = both.shape[1] // 2
    return both[:, :width] + both[:, width:]


def lane_iota(shape):
    return lax.broadcasted_iota(jnp.int32, shape, 1)


def row_iota(shape):
    return lax.broadcasted_iota(jnp.int32, shape, 0)


def neumann(neg, order, eye):
    power = [dot3(n, n) for n in neg]
    total = [eye + n for n in neg]
    size = 2
    while size < order:
        if size * 2 >= order:
            total = [x + dot3(x, p) for x, p in zip(total, power)]
        else:
            both = [dot3(jnp.concatenate([x, p], axis=0), p) for x, p in zip(total, power)]
            total = [x + b[:TILE] for x, b in zip(total, both)]
            power = [b[TILE:] for b in both]
        size *= 2
    return total


def inverses(mats):
    shape = (TILE, TILE)
    row, col = row_iota(shape), lane_iota(shape)
    eye = (row == col).astype(F32)
    diag = row // BASE == col // BASE
    inner = neumann([jnp.where(diag, -a, 0.0) for a in mats], BASE, eye)
    parts = [split(x) for x in inner]
    outer = [-dot3(p, jnp.where(diag, 0.0, a)) for p, a in zip(parts, mats)]
    return [dot3(y, p) for y, p in zip(neumann(outer, TILE // BASE, eye), parts)]


def kernel(
    nz, nd, q_ref, k_ref, v_ref, g_ref, b_ref, owner_ref, start_ref, gain_ref, out_ref,
    buf, bbuf, betas, place, stage, segcol, masks, growth, keyinv, keystate, keyend, halves,
    inverse, update, states,
    send_sem, recv_sem, bsend_sem, brecv_sem, osend_sem, orecv_sem,
):
    me = lax.axis_index("head")
    doc = lax.axis_index("doc")
    heads, _, rowtok, _ = buf.shape
    tok = q_ref.shape[0]
    nblk = rowtok // BLOCK
    cap = 2 * nblk // RUNS
    capt = cap * BLOCK
    tiles = rowtok // TILE
    refs = (q_ref, k_ref, v_ref, g_ref)

    barrier = pltpu.get_barrier_semaphore()
    count = 0
    for step in range(1, nz):
        pl.semaphore_signal(
            barrier, inc=1, device_id={"head": lax.rem(me + step, nz)}, device_id_type=MESH
        )
        count += 1
    peers = sorted({s % nd for s in range(1, RUNS)} | {(-s) % nd for s in range(1, RUNS)})
    for step in peers:
        pl.semaphore_signal(
            barrier, inc=1, device_id={"doc": lax.rem(doc + step, nd)}, device_id_type=MESH
        )
        count += 1
    pl.semaphore_wait(barrier, count)

    mine = pl.ds(pl.multiple_of(me * tok, tok), tok)

    def incoming(step, head, which):
        partner = lax.rem(me + step, nz)
        column = pl.ds(pl.multiple_of((partner * heads + head) * WIDTH, WIDTH), WIDTH)
        source = refs[which].at[:, column]
        target = buf.at[head, which, mine, :]
        if step == 0:
            return pltpu.make_async_copy(source, target, recv_sem.at[0, head, which])
        return pltpu.make_async_remote_copy(
            src_ref=source,
            dst_ref=target,
            send_sem=send_sem.at[step, head, which],
            recv_sem=recv_sem.at[step, head, which],
            device_id={"head": partner},
            device_id_type=MESH,
        )

    def incoming_beta(step):
        if step == 0:
            return pltpu.make_async_copy(b_ref, bbuf.at[me], brecv_sem.at[0])
        return pltpu.make_async_remote_copy(
            src_ref=b_ref,
            dst_ref=bbuf.at[me],
            send_sem=bsend_sem.at[step],
            recv_sem=brecv_sem.at[step],
            device_id={"head": lax.rem(me + step, nz)},
            device_id_type=MESH,
        )

    def outgoing(run, head):
        rows = pl.ds(run * capt, capt)
        return pltpu.make_async_remote_copy(
            src_ref=stage.at[head, rows, :],
            dst_ref=out_ref.at[rows, pl.ds(pl.multiple_of(head * WIDTH, WIDTH), WIDTH)],
            send_sem=osend_sem.at[run, head],
            recv_sem=orecv_sem.at[run, head],
            device_id={"doc": lax.rem(doc + run, nd)},
            device_id_type=MESH,
        )

    for step in range(nz):
        incoming_beta(step).start()
    early = max(heads - 2, 0)
    order = [(head, which) for head in range(heads) for which in (1, 3)]
    order += [(head, which) for head in range(early) for which in (2, 0)]
    order += [(head, which) for which in (2, 0) for head in range(early, heads)]
    for head, which in order:
        for step in list(range(1, nz)) + [0]:
            incoming(step, head, which).start()

    here = row_iota((nd, nblk)) == doc
    owner = jnp.sum(jnp.where(here, owner_ref[...], 0), axis=0, keepdims=True)
    start = jnp.sum(jnp.where(here, start_ref[...], 0), axis=0, keepdims=True)
    eye_b = row_iota((nblk, nblk)) == lane_iota((nblk, nblk))
    owner_col = jnp.sum(jnp.where(eye_b, owner, 0), axis=1, keepdims=True)
    earlier = row_iota((nblk, nblk)) < lane_iota((nblk, nblk))
    rank = jnp.sum(jnp.where(earlier & (owner_col == owner), 1, 0), axis=0, keepdims=True)
    ahead = owner - doc
    ahead = jnp.where(ahead < 0, ahead + nd, ahead)
    slot = (ahead * cap + rank).astype(F32).astype(BF16)
    token_block = lane_iota((nblk, rowtok)) // BLOCK
    expand = (row_iota((nblk, rowtok)) == token_block).astype(F32).astype(BF16)
    slot_tok = bdot(slot, expand).astype(jnp.int32) * BLOCK + lane_iota((1, rowtok)) % BLOCK
    place[...] = (row_iota((RUNS * capt, rowtok)) == slot_tok).astype(F32).astype(BF16)
    upto = (row_iota((nblk, rowtok)) <= token_block).astype(F32).astype(BF16)
    seg_row = bdot(start.astype(F32).astype(BF16), upto)
    seg_col = jnp.sum(
        jnp.where(
            lane_iota((rowtok, nblk)) <= row_iota((rowtok, nblk)) // BLOCK, start.astype(F32), 0.0
        ),
        axis=1,
        keepdims=True,
    )
    segcol[...] = jnp.broadcast_to(seg_col, (rowtok, WIDTH))
    shape = (TILE, TILE)
    for tile in range(tiles):
        lo = tile * TILE
        same = seg_col[lo : lo + TILE] == seg_row[:, lo : lo + TILE]
        masks[tile, 0] = (same & (row_iota(shape) > lane_iota(shape))).astype(F32)
        masks[tile, 1] = (same & (row_iota(shape) >= lane_iota(shape))).astype(F32)

    for step in range(nz):
        if step == 0:
            incoming_beta(0).wait()
        else:
            incoming_beta(step).wait_recv()

    eye_tok = (row_iota((tok, tok)) == lane_iota((tok, tok))).astype(F32).astype(BF16)
    for step in range(nz):
        turned = bdot(eye_tok, bbuf[step], NT)
        betas[step * tok : (step + 1) * tok, :] = jax.nn.sigmoid(turned)

    def arrive(head, which):
        incoming(0, head, which).wait()
        for step in range(1, nz):
            incoming(step, head, which).wait_recv()

    def beta_of(head):
        values = betas[...]
        mine_here = lane_iota(values.shape) == me * heads + head
        return jnp.sum(jnp.where(mine_here, values, 0.0), axis=1, keepdims=True)

    def before(tile):
        return segcol[tile * TILE - 1 : tile * TILE, :]

    def final(tile):
        return segcol[(tile + 1) * TILE - 1 : (tile + 1) * TILE, :]

    group = 2 if heads % 2 == 0 else 1

    def keys_part(index, carry):
        lower = (row_iota(shape) >= lane_iota(shape)).astype(F32).astype(BF16)
        where, amats = [], []
        for member in range(group):
            head = index * group + member
            arrive(head, 1)
            arrive(head, 3)
            beta = beta_of(head)
            for tile in range(tiles):
                rows = pl.ds(tile * TILE, TILE)
                seg = segcol[rows, :]
                key = buf[head, 1, rows, :].astype(F32)
                key = key * lax.rsqrt(jnp.sum(key * key, axis=-1, keepdims=True) + 1e-06)
                cumul = bdot(lower, buf[head, 3, rows, :])
                half = 0.5 * cumul[TILE - 1 :, :]
                grow = jnp.exp(cumul - half)
                middle = jnp.exp(half)
                kg, ki = key * grow, key * jnp.exp(half - cumul)
                amat = dot3(kg, ki, NT)
                amat = jnp.where(masks[tile, 0] > 0.0, amat, 0.0)
                amats.append(amat * beta[tile * TILE : (tile + 1) * TILE])
                where.append((head, rows))
                growth[head, rows, :] = grow
                keyinv[head, rows, :] = ki
                halves[head, tile] = jnp.broadcast_to(middle, (8, WIDTH))
                if tile > 0:
                    keystate[head, rows, :] = kg * ((seg == before(tile)).astype(F32) * middle)
                if tile < tiles - 1:
                    keyend[head, rows, :] = ki * ((seg == final(tile)).astype(F32) * middle)
        for (head, rows), inv in zip(where, inverses(amats)):
            inverse[head, rows, :] = inv
        return carry

    lax.fori_loop(0, heads // group, keys_part, 0)

    def values_part(index, carry):
        members = [index]
        state = [None]
        for head in members:
            arrive(head, 2)
        beta = [beta_of(head) for head in members]
        for tile in range(tiles):
            lo = tile * TILE
            rows = pl.ds(lo, TILE)
            right = [buf[head, 2, rows, :].astype(F32) for head in members]
            if tile > 0:
                right = [
                    r - dot3(keystate[head, rows, :], s)
                    for r, head, s in zip(right, members, state)
                ]
            new = [
                dot3(inverse[head, rows, :], b[lo : lo + TILE] * r)
                for head, b, r in zip(members, beta, right)
            ]
            for head, n in zip(members, new):
                update[head, rows, :] = n
            if tile < tiles - 1:
                added = [dot3(keyend[head, rows, :], n, TN) for head, n in zip(members, new)]
                if tile > 0:
                    eye = row_iota(shape) == lane_iota(shape)
                    unbroken = (final(tile) == before(tile)).astype(F32)
                    for place_in, head in enumerate(members):
                        middle = halves[head, tile, 0:1, :]
                        scale = middle * middle * unbroken
                        scale = jnp.sum(jnp.where(eye, scale, 0.0), axis=1, keepdims=True)
                        added[place_in] = added[place_in] + scale * state[place_in]
                state = added
                for head, s in zip(members, state):
                    states[head, tile] = s
        return carry


    def queries_part(head, carry):
        arrive(head, 0)
        gain = gain_ref[:, pl.ds(pl.multiple_of(head * WIDTH, WIDTH), WIDTH)]
        outs = []
        for tile in range(tiles):
            rows = pl.ds(tile * TILE, TILE)
            query = buf[head, 0, rows, :].astype(F32)
            query = (
                query
                * lax.rsqrt(jnp.sum(query * query, axis=-1, keepdims=True) + 1e-06)
                * WIDTH ** (-0.5)
            )
            qg = query * growth[head, rows, :]
            scores = dot3(qg, keyinv[head, rows, :], NT)
            scores = jnp.where(masks[tile, 1] > 0.0, scores, 0.0)
            result = dot3(scores, update[head, rows, :])
            if tile > 0:
                first = (segcol[rows, :] == before(tile)).astype(F32) * halves[head, tile, 0:1, :]
                result = result + dot3(qg * first, states[head, tile - 1])
            norm = lax.rsqrt(jnp.mean(result * result, axis=-1, keepdims=True) + 1e-05)
            outs.append((result * norm * gain).astype(BF16))
        placed = bdot(place[...], jnp.concatenate(outs, axis=0)).astype(BF16)
        stage[head] = placed
        for run in range(RUNS - 1, 0, -1):
            outgoing(run, head).start()
        out_ref[0:capt, pl.ds(pl.multiple_of(head * WIDTH, WIDTH), WIDTH)] = placed[:capt]
        return carry

    def both_parts(head, carry):
        return queries_part(head, values_part(head, carry))

    lax.fori_loop(0, early, both_parts, 0)
    lax.fori_loop(early, heads, values_part, 0)
    lax.fori_loop(early, heads, queries_part, 0)

    def finish(head, carry):
        for step in range(1, nz):
            for which in range(4):
                incoming(step, head, which).wait_send()
        for run in range(1, RUNS):
            outgoing(run, head).wait()
        return carry

    for step in range(1, nz):
        incoming_beta(step).wait_send()
    lax.fori_loop(0, heads, finish, 0)


def solution(mesh):
    nz, nd = mesh.shape["head"], mesh.shape["doc"]

    def local(queries, keys, values, log_decay, beta_logit, block_owner, block_start, gain):
        tok, channels = queries.shape
        heads = channels // WIDTH // nz
        rowtok = tok * nz
        slots = 2 * rowtok
        vmem = pl.BlockSpec(memory_space=pltpu.VMEM)
        return pl.pallas_call(
            functools.partial(kernel, nz, nd),
            out_shape=pltpu.VMEM((slots, heads * WIDTH), BF16),
            in_specs=[pl.BlockSpec(memory_space=pl.ANY)] * 4 + [vmem] * 4,
            out_specs=vmem,
            scratch_shapes=[
                pltpu.VMEM((heads, 4, rowtok, WIDTH), BF16),
                pltpu.VMEM((nz, beta_logit.shape[1], tok), BF16),
                pltpu.VMEM((rowtok, beta_logit.shape[1]), F32),
                pltpu.VMEM((slots, rowtok), BF16),
                pltpu.VMEM((heads, slots, WIDTH), BF16),
                pltpu.VMEM((rowtok, WIDTH), F32),
                pltpu.VMEM((rowtok // TILE, 2, TILE, TILE), F32),
                pltpu.VMEM((heads, rowtok, WIDTH), F32),
                pltpu.VMEM((heads, rowtok, WIDTH), F32),
                pltpu.VMEM((heads, rowtok, WIDTH), F32),
                pltpu.VMEM((heads, rowtok, WIDTH), F32),
                pltpu.VMEM((heads, rowtok // TILE, 8, WIDTH), F32),
                pltpu.VMEM((heads, rowtok, WIDTH), F32),
                pltpu.VMEM((heads, rowtok, WIDTH), F32),
                pltpu.VMEM((heads, rowtok // TILE, WIDTH, WIDTH), F32),
                pltpu.SemaphoreType.DMA((nz, heads, 4)),
                pltpu.SemaphoreType.DMA((nz, heads, 4)),
                pltpu.SemaphoreType.DMA((nz,)),
                pltpu.SemaphoreType.DMA((nz,)),
                pltpu.SemaphoreType.DMA((RUNS, heads)),
                pltpu.SemaphoreType.DMA((RUNS, heads)),
            ],
            compiler_params=pltpu.CompilerParams(
                collective_id=0, has_side_effects=True, vmem_limit_bytes=60 * 1024 * 1024
            ),
            name="delta",
        )(
            queries, keys, values, log_decay, beta_logit.T, block_owner, block_start,
            gain.reshape(1, -1),
        )

    return jax.shard_map(
        local,
        mesh=mesh,
        in_specs=(P(("doc", "head"), None),) * 5 + (P(), P(), P("head")),
        out_specs=P("doc", "head"),
        check_vma=False,
    )
```
